32 devices in a mesh: seq: 16 (over z, y, x), head: 2 (over core).
Axes of the slice: x: 2, y: 2, z: 4, core: 2. Of those that a mesh axis runs over, the one named last changes fastest.
Arguments:
- hidden: bfloat16 [8192, 1536], P('seq'), may hold values from -6 to 6
- cotangent: bfloat16 [8192, 1536], P('seq'), may hold values from -6 to 6
- z_proj: bfloat16 [1536, 3072], P('seq', 'head'), may hold values from -0.15625 to 0.15625
- x_proj: bfloat16 [1536, 3072], P('seq', 'head'), may hold values from -0.15625 to 0.15625
- bc_proj: bfloat16 [1536, 256], P('seq', 'head'), may hold values from -0.15625 to 0.15625
- dt_proj: bfloat16 [1536, 48], P('seq', 'head'), may hold values from -0.15625 to 0.15625
- out_proj: bfloat16 [1536, 3072], P('seq', 'head'), may hold values from -0.109375 to 0.109375
- conv_x: float32 [4, 3072], P(None, 'head'), may hold values from -2 to 2
- conv_x_bias: float32 [3072], P('head'), may hold values from -2 to 2
- conv_bc: float32 [4, 256], P(None, 'head'), may hold values from -2 to 2
- conv_bc_bias: float32 [256], P('head'), may hold values from -2 to 2
- dt_bias: float32 [48], P('head'), may hold values from -9 to -1
- a_log: float32 [48], P('head'), may hold values from -2.5 to 0.5
- d_skip: float32 [48], P('head'), may hold values from 0.5 to 1.5
- norm_gain: float32 [1536], replicated, may hold values from 0.1 to 1.9
- gate_gain: float32 [3072], P('head'), may hold values from 0.1 to 1.9
- lengths: int32 [2, 8], replicated, may hold values from 1 to 4, 16 in all within a row
- dealing: int32 [2, 16], replicated, may hold values from 0 to 15, each once within a row
Outputs:
- block_out: bfloat16 [8192, 1536], P('seq', 'head')
- grad_hidden: float32 [8192, 1536], P('seq', 'head')
- grad_z_proj: float32 [1536, 3072], P('seq', 'head')
- grad_x_proj: float32 [1536, 3072], P('seq', 'head')
- grad_bc_proj: float32 [1536, 256], P('seq', 'head')
- grad_dt_proj: float32 [1536, 48], P('seq', 'head')
- grad_out_proj: float32 [1536, 3072], P('seq', 'head')
- grad_conv_x: float32 [4, 3072], P(None, 'head')
- grad_conv_x_bias: float32 [3072], P('head')
- grad_conv_bc: float32 [4, 256], P(None, 'head')
- grad_conv_bc_bias: float32 [256], P('head')
- grad_dt_bias: float32 [48], P('head')
- grad_a_log: float32 [48], P('head')
- grad_d_skip: float32 [48], P('head')
- grad_norm_gain: float32 [1536], P('head')
- grad_gate_gain: float32 [3072], P('head')
The draws below stay inside these ranges and needn't reach their ends.
Inputs may be any that keep to these rules, and one draw needn't show every extreme that they name: `lengths`: each row sums to 16 runs of 256 rows; its largest entry is 4. `dealing`: each row is a permutation of the seq indices.
All inputs are finite; a program needn't handle non-finite values.
Results may differ from the reference program's by a relative error of at most 0.02.
Values may be sent and summed in bfloat16 or wider, within the bound.
No kernel may reach another device: no remote copies, remote signals or barrier semaphores. Data moves between devices by JAX's collectives and lax.ppermute only.
A program may use at most 192 MiB of HBM per device.

```python
import math
from functools import partial
import jax
import jax.numpy as jnp
import numpy as np
from jax import lax

MODEL_WIDTH = 1536
HEADS = 48
HDIM = 64
STATE = 128
BLOCK = 256
MB = 2
RUN = 256
INNER = 3072
RUNS = 16
SEQS = 8
LONGEST = 4
TOKENS = 8192
N_SEQ = 16


def levels(rng, dims, cuts, least, top_value):
    def one(dim, blocks):
        draws = jax.random.uniform(jax.random.fold_in(jax.random.fold_in(rng, 6), dim), (blocks,), jnp.float32, least / len(cuts), top_value / len(cuts))
        return jnp.repeat(jnp.exp(draws), dims[dim] // blocks).reshape((-1,) + (1,) * (len(dims) - dim - 1))

    factor_of = one(*cuts[0])
    for cut in cuts[1:]:
        factor_of = factor_of * one(*cut)
    return factor_of


def length_profile(amount, total, limit, lean):
    weights = [(1 << 20) // math.isqrt(rank ** lean) + 1 for rank in range(2, amount + 1)]
    spare, counts = total - limit - (amount - 1), [1] * (amount - 1)
    while spare > 0:
        candidates = [i for i in range(amount - 1) if counts[i] < limit]
        mass, left = sum([weights[i] for i in candidates]), spare
        for i in candidates:
            addition = min(limit - counts[i], max(1, left * weights[i] // mass), spare)
            counts[i] = counts[i] + addition
            spare = spare - addition
    return np.array([limit] + counts)


def ragged_sizes(stream_key, number_of, total, bound, lean):
    if number_of == 2:
        one = jax.random.randint(stream_key, (), max(1, total - bound), min(bound, total - 1) + 1)
        return jnp.stack([one, total - one])
    sizes = jnp.asarray(length_profile(number_of, total, bound, lean), jnp.int32)
    couples = (number_of - 1) // 2
    giver, receiver = sizes[1:1 + 2 * couples:2], sizes[2:2 + 2 * couples:2]
    margin = jnp.minimum(giver - 1, bound - receiver)
    moved = jax.random.randint(jax.random.fold_in(stream_key, 1), (couples,), 0, 1 << 20) % (margin + 1)
    sizes = sizes.at[1:1 + 2 * couples:2].set(giver - moved).at[2:2 + 2 * couples:2].set(receiver + moved)
    return sizes[jax.random.permutation(jax.random.fold_in(stream_key, 2), number_of)]


def normal_values(key, extent, scale, reach, cuts=(), kind=jnp.bfloat16):
    entries = scale * jax.random.normal(key, extent, jnp.float32)
    if cuts:
        entries = entries * levels(key, extent, cuts, -0.22, 0.18)
    return jnp.clip(entries, -reach, reach).astype(kind)


def setup_inputs(seed: int = 0) -> dict:
    seeds = jax.random.split(jax.random.key(seed), 19)
    return {
        "hidden": normal_values(seeds[0], (TOKENS, MODEL_WIDTH), 1.0, 6.0, ((0, 16),)),
        "cotangent": normal_values(seeds[1], (TOKENS, MODEL_WIDTH), 1.0, 6.0, ((0, 16),)),
        "z_proj": normal_values(seeds[2], (MODEL_WIDTH, INNER), MODEL_WIDTH ** -0.5, 0.15625, ((0, 16), (1, 2))),
        "x_proj": normal_values(seeds[3], (MODEL_WIDTH, INNER), MODEL_WIDTH ** -0.5, 0.15625, ((0, 16), (1, 2))),
        "bc_proj": normal_values(seeds[4], (MODEL_WIDTH, 2 * STATE), MODEL_WIDTH ** -0.5, 0.15625, ((0, 16), (1, 2))),
        "dt_proj": normal_values(seeds[5], (MODEL_WIDTH, HEADS), MODEL_WIDTH ** -0.5, 0.15625, ((0, 16), (1, 2))),
        "out_proj": normal_values(seeds[6], (MODEL_WIDTH, INNER), INNER ** -0.5, 0.109375, ((0, 16), (1, 2))),
        "conv_x": normal_values(seeds[7], (4, INNER), 0.5, 2.0, ((1, 2),), jnp.float32),
        "conv_x_bias": normal_values(seeds[8], (INNER,), 0.5, 2.0, ((0, 2),), jnp.float32),
        "conv_bc": normal_values(seeds[9], (4, 2 * STATE), 0.5, 2.0, ((1, 2),), jnp.float32),
        "conv_bc_bias": normal_values(seeds[10], (2 * STATE,), 0.5, 2.0, ((0, 2),), jnp.float32),
        "dt_bias": jnp.clip(-9.0 + 8.0 * jax.random.uniform(seeds[11], (HEADS,), jnp.float32) ** levels(seeds[11], (HEADS,), ((0, 2),), -0.2, 0.2), -9.0, -1.0),
        "a_log": jnp.clip(-2.5 + 3.0 * jax.random.uniform(seeds[12], (HEADS,), jnp.float32) ** levels(seeds[12], (HEADS,), ((0, 2),), -0.2, 0.2), -2.5, 0.5),
        "d_skip": jnp.clip(0.5 + 1.0 * jax.random.uniform(seeds[13], (HEADS,), jnp.float32) ** levels(seeds[13], (HEADS,), ((0, 2),), -0.2, 0.2), 0.5, 1.5),
        "norm_gain": jnp.clip(1.0 + 0.18 * jax.random.normal(seeds[14], (MODEL_WIDTH,), jnp.float32), 0.1, 1.9),
        "gate_gain": jnp.clip(1.0 + 0.18 * jax.random.normal(seeds[15], (INNER,), jnp.float32), 0.1, 1.9),
        "lengths": jax.vmap(lambda own: ragged_sizes(own, SEQS, RUNS, LONGEST, 1))(jax.random.split(seeds[16], MB)).reshape((MB, SEQS)).astype(jnp.int32),
        "dealing": jax.vmap(lambda own: jax.random.permutation(own, RUNS))(jax.random.split(seeds[17], MB)).reshape((MB, RUNS)).astype(jnp.int32),
    }


EPSILON = 1e-05
HIGHEST = lax.Precision.HIGHEST

@jax.custom_vjp
def low(v):
    return lax.optimization_barrier(v.astype(jnp.bfloat16)).astype(jnp.float32)

@jax.custom_vjp
def low_back(v):
    return v

def low_keep(v):
    return (low(v), None)

def low_pass(kept, grad):
    return (grad,)

def back_keep(v):
    return (v, None)

def back_low(kept, grad):
    return (low(grad),)
low.defvjp(low_keep, low_pass)
low_back.defvjp(back_keep, back_low)

def matmul_hi(left_op, right_op):
    return jnp.dot(left_op, right_op, precision=HIGHEST)

def block_step(params, carry, inputs):
    z_proj, x_proj, bc_proj, dt_proj, out_proj, conv_taps, conv_bias, dt_bias, a_log, d_skip, norm_gain, gate_gain = params
    state_now, conv_tail = carry
    tokens, reset_flag = inputs
    keep_in = 1.0 - reset_flag
    reciprocal_root_mean = lax.rsqrt(lax.optimization_barrier(jnp.mean(tokens * tokens, axis=1, keepdims=True)) + EPSILON)
    normed = low(tokens * reciprocal_root_mean * norm_gain)
    gate_val = low(low_back(matmul_hi(normed, z_proj)))
    x_in = low(low_back(matmul_hi(normed, x_proj)))
    bc_in = low(low_back(matmul_hi(normed, bc_proj)))
    dt_in = low_back(matmul_hi(normed, dt_proj))
    conv_in = jnp.concatenate([x_in, bc_in], axis=1)
    extended = jnp.concatenate([conv_tail * keep_in, conv_in], axis=0)
    conv_pre = conv_bias
    for tap_at in range(4):
        conv_pre = conv_pre + conv_taps[tap_at] * extended[tap_at:tap_at + BLOCK]
    conv_act = jax.nn.silu(conv_pre)
    x_mix = low(conv_act[:, :INNER])
    bc_val = low(conv_act[:, INNER:])
    b_mat = bc_val[:, :STATE]
    c_mat = bc_val[:, STATE:]
    dt_val = jax.nn.softplus(dt_in + dt_bias)
    rate_val = dt_val * -jnp.exp(a_log)
    cum_rate = jnp.cumsum(rate_val, axis=0)
    start_state = state_now * keep_in
    scores = low_back(matmul_hi(c_mat, b_mat.T))
    lower_tri = jnp.arange(BLOCK)[:, None] >= jnp.arange(BLOCK)[None, :]
    cum_heads = cum_rate.T
    exponent = jnp.where(lower_tri[None], cum_heads[:, :, None] - cum_heads[:, None, :], 0.0)
    decay_mask = jnp.exp(exponent) * lower_tri[None]
    mix_wt = low(scores[None] * decay_mask * dt_val.T[:, None, :])
    heads_x = x_mix.reshape(BLOCK, HEADS, HDIM)
    inner_out = jnp.einsum('hij,jhp->ihp', mix_wt, heads_x, precision=HIGHEST)
    outer_out = jnp.exp(cum_rate)[:, :, None] * jnp.einsum('in,hpn->ihp', c_mat, start_state, precision=HIGHEST)
    ssd_out = low_back((inner_out + outer_out + d_skip[None, :, None] * heads_x).reshape(BLOCK, INNER))
    weight_end = jnp.exp(cum_rate[-1:] - cum_rate) * dt_val
    new_state = jnp.exp(cum_rate[-1])[:, None, None] * start_state + jnp.einsum('jhp,jn->hpn', weight_end[:, :, None] * heads_x, b_mat, precision=HIGHEST)
    gated = ssd_out * jax.nn.silu(gate_val)
    inv_gate = lax.rsqrt(lax.optimization_barrier(jnp.mean(gated * gated, axis=1, keepdims=True)) + EPSILON)
    branch = low(gated * inv_gate * gate_gain)
    block_rows = tokens + matmul_hi(branch, out_proj.T)
    return ((new_state, conv_in[BLOCK - 3:]), block_rows)

def run_packed(params, tokens, resets):
    step_fn = jax.checkpoint(partial(block_step, params))
    start = (jnp.zeros((HEADS, HDIM, STATE), jnp.float32), jnp.zeros((3, INNER + 2 * STATE), jnp.float32))
    _, result = lax.scan(step_fn, start, (tokens.reshape(-1, BLOCK, MODEL_WIDTH), resets))
    return result.reshape(-1, MODEL_WIDTH)

def forward(lengths, dealing, hidden, z_proj, x_proj, bc_proj, dt_proj, out_proj, conv_x, conv_x_bias, conv_bc, conv_bc_bias, dt_bias, a_log, d_skip, norm_gain, gate_gain):
    run_order = jnp.arange(RUNS, dtype=jnp.int32)
    run_ends = jnp.cumsum(lengths, axis=1)
    run_start = jnp.any((run_ends - lengths)[:, :, None] == run_order[None, None, :], axis=1)
    per_run = RUN // BLOCK
    first_block = jnp.arange(RUNS * per_run, dtype=jnp.int32) % per_run == 0
    resets = (jnp.repeat(run_start, per_run, axis=1) & first_block[None]).astype(jnp.float32)
    grid = hidden.reshape(N_SEQ, MB, RUN, MODEL_WIDTH)
    micro_ids = jnp.arange(MB, dtype=jnp.int32)
    packed = grid[dealing, micro_ids[:, None]].reshape(MB, RUNS * RUN, MODEL_WIDTH)
    conv_taps = jnp.concatenate([conv_x, conv_bc], axis=1)
    conv_bias = jnp.concatenate([conv_x_bias, conv_bc_bias])
    params = (z_proj, x_proj, bc_proj, dt_proj, out_proj, conv_taps, conv_bias, dt_bias, a_log, d_skip, norm_gain, gate_gain)
    result = lax.map(lambda pair: run_packed(params, pair[0], pair[1]), (packed, resets))
    result = result.reshape(MB, RUNS, RUN, MODEL_WIDTH)
    inverse = jnp.argsort(dealing, axis=1).astype(jnp.int32)
    placed = result[micro_ids[None, :], inverse.T]
    return placed.reshape(TOKENS, MODEL_WIDTH)

def reference(hidden, cotangent, z_proj, x_proj, bc_proj, dt_proj, out_proj, conv_x, conv_x_bias, conv_bc, conv_bc_bias, dt_bias, a_log, d_skip, norm_gain, gate_gain, lengths, dealing):
    floats = (hidden, z_proj, x_proj, bc_proj, dt_proj, out_proj, conv_x, conv_x_bias, conv_bc, conv_bc_bias, dt_bias, a_log, d_skip, norm_gain, gate_gain)
    floats = tuple((item.astype(jnp.float32) for item in floats))
    result, pull = jax.vjp(partial(forward, lengths, dealing), *floats)
    grads = pull(cotangent.astype(jnp.float32))
    return (result.astype(jnp.bfloat16), grads[0], grads[1], grads[2], grads[3], grads[4], grads[5], grads[6], grads[7], grads[8], grads[9], grads[10], grads[11], grads[12], grads[13], grads[14])
```

```python
import jax
import jax.numpy as jnp
from jax import lax
from jax.experimental import pallas as pl
from jax.experimental.pallas import tpu as pltpu
from jax.sharding import PartitionSpec as P

MODEL_WIDTH = 1536
HDIM = 64
STATE = 128
BLOCK = 256
INNER = 3072
HALO = 8
LANES = 128
EPSILON = 1e-05

F32 = jnp.float32
BF16 = jnp.bfloat16


def dot_nn(left, right):
    return lax.dot_general(left, right, (((1,), (0,)), ((), ())), preferred_element_type=F32)


def dot_nt(left, right):
    return lax.dot_general(left, right, (((1,), (1,)), ((), ())), preferred_element_type=F32)


def dot_tn(left, right):
    return lax.dot_general(left, right, (((0,), (0,)), ((), ())), preferred_element_type=F32)


def split_bf16(value, parts):
    pieces = []
    for _ in range(parts - 1):
        upper = value.astype(BF16)
        pieces.append(upper)
        value = value - upper.astype(F32)
    pieces.append(value.astype(BF16))
    return pieces


def head_rows(first_lane, width):
    lane = lax.broadcasted_iota(jnp.int32, (LANES, width), 1) + first_lane
    row = lax.broadcasted_iota(jnp.int32, (LANES, width), 0)
    return (lax.shift_right_logical(lane, 6) == row).astype(F32).astype(BF16)


def head_cols(first_lane, width):
    lane = lax.broadcasted_iota(jnp.int32, (width, LANES), 0) + first_lane
    col = lax.broadcasted_iota(jnp.int32, (width, LANES), 1)
    return (lax.shift_right_logical(lane, 6) == col).astype(F32).astype(BF16)


def spread(pieces, marks):
    total = dot_nn(pieces[0], marks)
    for piece in pieces[1:]:
        total = total + dot_nn(piece, marks)
    return total


def gather_heads(value, marks_t):
    upper, lower = split_bf16(value, 2)
    return dot_nn(upper, marks_t) + dot_nn(lower, marks_t)


def tri_rows(size, reverse=False):
    row = lax.broadcasted_iota(jnp.int32, (size, size), 0)
    col = lax.broadcasted_iota(jnp.int32, (size, size), 1)
    return (row <= col) if reverse else (row >= col)


def lane_tile(width):
    return 256 if width % 256 == 0 else LANES


def load_states(dst, src):
    count, _, rows, _ = src.shape
    for at in range(count):
        dst[at * rows : (at + 1) * rows, :] = src[at, 0].astype(F32)


def assemble(blocks, places):
    count = len(blocks)
    rows, cols = blocks[0].shape

    def body(place_ref, *refs):
        out, sems = refs[count], refs[count + 1]
        copies = [
            pltpu.make_async_copy(refs[at], out.at[place_ref[at]], sems.at[at]) for at in range(count)
        ]
        for copy in copies:
            copy.start()
        for copy in copies:
            copy.wait()

    return pl.pallas_call(
        body,
        grid_spec=pltpu.PrefetchScalarGridSpec(
            num_scalar_prefetch=1,
            grid=(1,),
            in_specs=[pl.BlockSpec(memory_space=pl.ANY)] * count,
            out_specs=pl.BlockSpec((count, rows, cols), lambda i, *_: (0, 0, 0)),
            scratch_shapes=[pltpu.SemaphoreType.DMA((count,))],
        ),
        out_shape=jax.ShapeDtypeStruct((count, rows, cols), BF16),
        name="assemble",
    )(places, *blocks).reshape(count * rows, cols)


def take_apart(grad, places, n):
    planes = n // 4
    n_even, n_odd = (planes + 1) // 2, planes // 2
    rows, cols = grad.shape[0] // n, grad.shape[1]
    shapes = [
        (n_even, 2, rows, cols),
        (n_even, rows, cols),
        (n_even, rows, cols),
        (n_odd, 2, rows, cols),
        (n_odd, rows, cols),
        (n_odd, rows, cols),
    ]

    def body(place_ref, src, *refs):
        outs, sems = refs[:6], refs[6]
        copies = []
        for plane in range(planes):
            at = plane // 2
            for near in range(4):
                step_y, step_x = near // 2, near % 2
                if plane % 2 == 0:
                    dst = outs[0].at[at, step_y] if step_x else outs[1 + step_y].at[at]
                else:
                    dst = outs[3].at[at, step_x] if step_y else outs[4 + step_x].at[at]
                index = plane * 4 + near
                copies.append(
                    pltpu.make_async_copy(src.at[place_ref[index]], dst, sems.at[index])
                )
        for copy in copies:
            copy.start()
        for copy in copies:
            copy.wait()

    return pl.pallas_call(
        body,
        grid_spec=pltpu.PrefetchScalarGridSpec(
            num_scalar_prefetch=1,
            grid=(1,),
            in_specs=[pl.BlockSpec((n, rows, cols), lambda i, *_: (0, 0, 0))],
            out_specs=[pl.BlockSpec(memory_space=pl.ANY)] * 6,
            scratch_shapes=[pltpu.SemaphoreType.DMA((n,))],
        ),
        out_shape=[jax.ShapeDtypeStruct(shape, BF16) for shape in shapes],
        name="take_apart",
    )(places, grad.reshape(n, rows, cols))


def row_block(rows, cols):
    return pl.BlockSpec((rows, cols), lambda m, *_: (m, 0))


def lead_block(rows, cols):
    return pl.BlockSpec((1, rows, cols), lambda m, *_: (m, 0, 0))


def whole_block(rows, cols):
    return pl.BlockSpec((rows, cols), lambda m, *_: (0, 0))


def state_block(n, nb, cols):
    return pl.BlockSpec((n, 1, nb, cols), lambda m, *_: (0, m, 0, 0))


def shape_of(shape, dtype):
    return jax.ShapeDtypeStruct(shape, dtype)


def conv_forward(scratch, base, taps, bias):
    pre = bias
    for tap_at in range(4):
        pre = pre + taps[tap_at : tap_at + 1] * scratch[base + 5 + tap_at : base + 5 + tap_at + BLOCK, :]
    return pre


def prep_kernel(keep_ref, bc_ref, dtin_ref, taps_ref, bias_ref, dtb_ref, neg_ref,
                bcin_ref, bcact_ref, dt_ref, cs_ref, sig_ref, cst_ref, ext):
    keep = keep_ref[pl.program_id(0)]
    low = bc_ref[...].astype(BF16).astype(F32)
    ext[0:HALO, :] = low[0:HALO, :] * keep
    ext[HALO:, :] = low[HALO:, :]
    bcin_ref[...] = ext[...].astype(BF16)
    pre = conv_forward(ext, 0, taps_ref[...], bias_ref[...])
    bcact_ref[...] = (pre * jax.nn.sigmoid(pre)).astype(BF16)
    raw = dtin_ref[HALO:, :] + dtb_ref[...]
    dt = jnp.maximum(raw, 0.0) + jnp.log1p(jnp.exp(-jnp.abs(raw)))
    dt_ref[...] = dt
    sig_ref[...] = jax.nn.sigmoid(raw)
    rate = dt * neg_ref[...]
    lower = tri_rows(BLOCK).astype(F32).astype(BF16)
    cs = jnp.zeros_like(rate)
    for piece in reversed(split_bf16(rate, 3)):
        cs = cs + dot_nn(lower, piece)
    cs_ref[...] = cs
    cst_ref[0] = cs.T


def project_kernel(keep_ref, normed_ref, w_ref, taps_ref, bias_ref, xin_ref, xmix_ref, ext):
    micro = keep_ref.shape[0]
    span = BLOCK + HALO
    ext[...] = dot_nn(normed_ref[...], w_ref[...]).astype(BF16).astype(F32)
    for m in range(micro):
        ext[m * span : m * span + HALO, :] = ext[m * span : m * span + HALO, :] * keep_ref[m]
    xin_ref[...] = ext[...].astype(BF16)
    for m in range(micro):
        pre = conv_forward(ext, m * span, taps_ref[...], bias_ref[...])
        xmix_ref[m * BLOCK : (m + 1) * BLOCK, :] = (pre * jax.nn.sigmoid(pre)).astype(BF16)


def end_state_kernel(x_ref, b_ref, dt_ref, cs_ref, out_ref):
    width = x_ref.shape[1]
    count, _, nb, _ = out_ref.shape
    tile = lane_tile(width)
    b_t = b_ref[...].astype(F32).T.astype(BF16)
    dt_p = split_bf16(dt_ref[...], 2)
    cs_p = split_bf16(cs_ref[...], 3)
    for c0 in range(0, width, tile):
        marks = head_rows(c0, tile)
        cs_x = spread(cs_p, marks)
        weight = jnp.exp(cs_x[BLOCK - 1 : BLOCK, :] - cs_x) * spread(dt_p, marks)
        xw = (x_ref[:, c0 : c0 + tile].astype(F32) * weight).astype(BF16)
        state = dot_nn(b_t, xw)
        for at in range(count):
            out_ref[at, 0, :, c0 : c0 + tile] = state[at * nb : (at + 1) * nb, :].astype(BF16)


def scan_kernel(reverse, deal_ref, first_ref, s_ref, lam_ref, out_ref, decay):
    count, micro, nb, width = s_ref.shape
    tile = lane_tile(width)
    for m in range(micro):
        pieces = split_bf16(lam_ref[m], 3)
        for c0 in range(0, width, tile):
            decay[m * count : (m + 1) * count, c0 : c0 + tile] = jnp.exp(
                spread(pieces, head_rows(c0, tile))
            )
    for m in range(micro):

        def step(at, state, m=m):
            p = count - 1 - at if reverse else at
            q = deal_ref[m * count + p]
            gain = 1.0 - first_ref[m * count + p].astype(F32)
            factor = decay[pl.ds(m * count + q, 1), :]
            own = s_ref[q, m].astype(F32)
            if reverse:
                out_ref[q, m] = state.astype(BF16)
                return (factor * state + own) * gain
            state = state * gain
            out_ref[q, m] = state.astype(BF16)
            return factor * state + own

        lax.fori_loop(0, count, step, jnp.zeros((nb, width), F32))


def intra_kernel(x_ref, b_ref, c_ref, dt_ref, cs_ref, cst_ref, y_ref, cb):
    width = x_ref.shape[1]
    cb[...] = jnp.where(tri_rows(BLOCK), dot_nt(c_ref[...], b_ref[...]), 0.0)
    dt_p = split_bf16(dt_ref[...], 2)
    cs_p = split_bf16(cs_ref[...], 3)
    left = lax.broadcasted_iota(jnp.int32, (BLOCK, LANES), 1) < HDIM

    def pair(g, carry):
        lanes = pl.ds(pl.multiple_of(g * LANES, LANES), LANES)
        marks = head_rows(g * LANES, LANES)
        cs_x = spread(cs_p, marks)
        xd = (x_ref[:, lanes].astype(F32) * spread(dt_p, marks)).astype(BF16)
        ys = []
        for e in range(2):
            gap = cs_x[:, e * HDIM : e * HDIM + 1] - cst_ref[0, pl.ds(2 * g + e, 1), :]
            mix = (cb[...] * jnp.exp(jnp.minimum(gap, 0.0))).astype(BF16)
            ys.append(dot_nn(mix, xd))
        y_ref[:, lanes] = jnp.where(left, ys[0], ys[1])
        return carry

    lax.fori_loop(0, width // LANES, pair, 0)


def stats_kernel(yin_ref, x_ref, c_ref, cs_ref, s_ref, gate_ref, db_ref, gain_ref, skip_ref,
                 y_ref, stat_ref, states):
    width = x_ref.shape[1]
    tile = lane_tile(width)
    load_states(states, s_ref)
    cs_p = split_bf16(cs_ref[...], 3)
    c_mat = c_ref[...]
    squares = jnp.zeros((BLOCK, tile), F32)
    crosses = jnp.zeros((BLOCK, tile), F32)
    for c0 in range(0, width, tile):
        sl = slice(c0, c0 + tile)
        outer = dot_nn(c_mat, states[:, sl].astype(BF16))
        decay = jnp.exp(spread(cs_p, head_rows(c0, tile)))
        y = yin_ref[:, sl] + decay * outer + skip_ref[:, sl] * x_ref[:, sl].astype(F32)
        y_ref[:, sl] = y
        gate = gate_ref[:, sl].astype(F32)
        gated = y * (gate * jax.nn.sigmoid(gate))
        squares = squares + gated * gated
        crosses = crosses + gated * (db_ref[:, sl] * gain_ref[:, sl])
    stat_ref[:, 0:1] = jnp.sum(squares, axis=1, keepdims=True)
    stat_ref[:, 1:2] = jnp.sum(crosses, axis=1, keepdims=True)


def gate_kernel(y_ref, c_ref, cs_ref, gate_ref, db_ref, gain_ref, stat_ref,
                branch_ref, dy_ref, dgate_ref, gg_ref, out_ref):
    width = y_ref.shape[1]
    count, _, nb, _ = out_ref.shape
    tile = lane_tile(width)
    cs_p = split_bf16(cs_ref[...], 3)
    c_t = c_ref[...].astype(F32).T.astype(BF16)
    root = lax.rsqrt(stat_ref[:, 0:1] / INNER + EPSILON)
    shift = root * stat_ref[:, 1:2] / INNER
    for c0 in range(0, width, tile):
        sl = slice(c0, c0 + tile)
        y = y_ref[:, sl]
        gate = gate_ref[:, sl].astype(F32)
        sig = jax.nn.sigmoid(gate)
        act = gate * sig
        scaled = y * act * root
        d_branch = db_ref[:, sl]
        gain = gain_ref[:, sl]
        branch_ref[:, sl] = (scaled * gain).astype(BF16)
        gg_ref[0, :, sl] = jnp.sum(d_branch * scaled, axis=0, keepdims=True)
        d_gated = root * (d_branch * gain - scaled * shift)
        dy = (d_gated * act).astype(BF16)
        dy_ref[:, sl] = dy
        dgate_ref[:, sl] = (d_gated * y * (sig * (1.0 + gate * (1.0 - sig)))).astype(BF16)
        decay = jnp.exp(spread(cs_p, head_rows(c0, tile)))
        state = dot_nn(c_t, (dy.astype(F32) * decay).astype(BF16))
        for at in range(count):
            out_ref[at, 0, :, sl] = state[at * nb : (at + 1) * nb, :].astype(BF16)


def intra_back_kernel(x_ref, dy_ref, b_ref, c_ref, dt_ref, cs_ref, cst_ref, y_ref, s_ref, skip_ref,
                      dxp_ref, db_ref, dc_ref, dcs_ref, ddt_ref, gs_ref,
                      cbt, acc, states):
    width = x_ref.shape[1]
    upper = tri_rows(BLOCK, reverse=True)
    cbt[...] = jnp.where(upper, dot_nt(b_ref[...], c_ref[...]), 0.0)
    acc[...] = jnp.zeros_like(acc)
    load_states(states, s_ref)
    dt_p = split_bf16(dt_ref[...], 2)
    cs_p = split_bf16(cs_ref[...], 3)
    left = lax.broadcasted_iota(jnp.int32, (BLOCK, LANES), 1) < HDIM
    dc_ref[...] = jnp.zeros_like(dc_ref)
    dcs_ref[...] = jnp.zeros_like(dcs_ref)
    ddt_ref[...] = jnp.zeros_like(ddt_ref)

    def pair(g, carry):
        lanes = pl.ds(pl.multiple_of(g * LANES, LANES), LANES)
        marks = head_rows(g * LANES, LANES)
        marks_t = head_cols(g * LANES, LANES)
        cs_x = spread(cs_p, marks)
        dt_x = spread(dt_p, marks)
        xf = x_ref[:, lanes].astype(F32)
        xd = (xf * dt_x).astype(BF16)
        xdf = xd.astype(F32)
        dy = dy_ref[:, lanes]
        dyf = dy.astype(F32)
        us = []
        total = acc[...]
        for e in range(2):
            gap = cst_ref[0, pl.ds(2 * g + e, 1), :] - cs_x[:, e * HDIM : e * HDIM + 1]
            decay = jnp.exp(jnp.minimum(gap, 0.0))
            half = jnp.where(left if e == 0 else ~left, xdf, 0.0).astype(BF16)
            total = total + dot_nt(half, dy) * decay
            us.append(dot_nn((cbt[...] * decay).astype(BF16), dy))
        acc[...] = total
        u = jnp.where(left, us[0], us[1])
        skip = skip_ref[:, lanes]
        dc_ref[...] += dot_nt((dyf * jnp.exp(cs_x)).astype(BF16), states[:, lanes].astype(BF16))
        dxp_ref[:, lanes] = dt_x * u + skip * dyf
        dcs_ref[...] += gather_heads(dyf * (y_ref[:, lanes] - skip * xf) - xdf * u, marks_t)
        ddt_ref[...] += gather_heads(xf * u, marks_t)
        gs_ref[0, :, lanes] = jnp.sum(dyf * xf, axis=0, keepdims=True)
        return carry

    lax.fori_loop(0, width // LANES, pair, 0)
    dcb_t = jnp.where(upper, acc[...], 0.0)
    db_ref[...] = dot_nn(dcb_t.astype(BF16), c_ref[...])
    dc_ref[...] += dot_nn(dcb_t.T.astype(BF16), b_ref[...])


def conv_back(ext, pad, d_act, taps, bias, keep):
    pre = conv_forward(ext, 0, taps, bias)
    sig = jax.nn.sigmoid(pre)
    d_pre = d_act * (sig * (1.0 + pre * (1.0 - sig)))
    pad[HALO : HALO + BLOCK, :] = d_pre
    g_taps = [
        jnp.sum(d_pre * ext[5 + tap_at : 5 + tap_at + BLOCK, :], axis=0, keepdims=True)
        for tap_at in range(4)
    ]
    g_bias = jnp.sum(d_pre, axis=0, keepdims=True)
    span = BLOCK + HALO
    d_in = taps[0:1] * pad[3 : 3 + span, :]
    for tap_at in range(1, 4):
        d_in = d_in + taps[tap_at : tap_at + 1] * pad[3 - tap_at : 3 - tap_at + span, :]
    row = lax.broadcasted_iota(jnp.int32, d_in.shape, 0)
    return d_in * jnp.where(row < HALO, keep, 1.0), g_taps, g_bias


def state_back_kernel(keep_ref, x_ref, b_ref, dt_ref, cs_ref, sig_ref, neg_ref, s_ref, ds_ref, dxp_ref,
                      dbp_ref, dcp_ref, dcs_ref, ddt_ref, xin_ref, taps_ref, bias_ref,
                      dx_ref, dbc_ref, ddtin_ref, gt_ref, gb_ref, ga_ref, gd_ref,
                      states, d_states, ext, pad):
    width = x_ref.shape[1]
    tile = lane_tile(width)
    keep = keep_ref[pl.program_id(0)]
    load_states(states, s_ref)
    load_states(d_states, ds_ref)
    dt = dt_ref[...]
    cs = cs_ref[...]
    dt_p = split_bf16(dt, 2)
    cs_p = split_bf16(cs, 3)
    b_mat = b_ref[...]
    d_b = dbp_ref[...]
    d_wend = jnp.zeros((BLOCK, LANES), F32)
    d_lam = jnp.zeros((8, LANES), F32)
    pad[0:HALO, :] = jnp.zeros((HALO, tile), F32)
    pad[HALO + BLOCK :, :] = jnp.zeros((HALO, tile), F32)
    for c0 in range(0, width, tile):
        sl = slice(c0, c0 + tile)
        marks = head_rows(c0, tile)
        marks_t = head_cols(c0, tile)
        ds_low = d_states[:, sl].astype(BF16)
        along = dot_nn(b_mat, ds_low)
        cs_x = spread(cs_p, marks)
        lam_x = cs_x[BLOCK - 1 : BLOCK, :]
        weight = jnp.exp(lam_x - cs_x) * spread(dt_p, marks)
        xf = x_ref[:, sl].astype(F32)
        d_b = d_b + dot_nt((xf * weight).astype(BF16), ds_low)
        d_wend = d_wend + gather_heads(along * xf, marks_t)
        cross = jnp.sum(d_states[:, sl] * states[:, sl], axis=0, keepdims=True) * jnp.exp(lam_x)
        d_lam = d_lam + gather_heads(jnp.broadcast_to(cross, (8, tile)), marks_t)
        ext[...] = xin_ref[:, sl].astype(F32)
        d_in, g_taps, g_bias = conv_back(
            ext, pad, dxp_ref[:, sl] + weight * along, taps_ref[:, sl], bias_ref[:, sl], keep
        )
        dx_ref[:, sl] = d_in.astype(BF16)
        for tap_at in range(4):
            gt_ref[0, tap_at : tap_at + 1, sl] = g_taps[tap_at]
        gb_ref[0, :, sl] = g_bias
    dbc_ref[:, :STATE] = d_b.astype(BF16)
    dbc_ref[:, STATE:] = dcp_ref[...].astype(BF16)
    fade = jnp.exp(cs[BLOCK - 1 : BLOCK, :] - cs)
    end_gain = d_wend * (fade * dt)
    d_cs = dcs_ref[...] - end_gain
    last = jnp.sum(end_gain, axis=0, keepdims=True) + d_lam[0:1, :]
    row = lax.broadcasted_iota(jnp.int32, d_cs.shape, 0)
    d_cs = d_cs + jnp.where(row == BLOCK - 1, last, 0.0)
    upper = tri_rows(BLOCK, reverse=True).astype(F32).astype(BF16)
    d_rate = jnp.zeros_like(d_cs)
    for piece in reversed(split_bf16(d_cs, 3)):
        d_rate = d_rate + dot_nn(upper, piece)
    neg = neg_ref[...]
    d_in = (ddt_ref[...] + d_wend * fade + d_rate * neg) * sig_ref[...]
    ddtin_ref[0:HALO, :] = jnp.zeros((HALO, LANES), BF16)
    ddtin_ref[HALO:, :] = d_in.astype(BF16)
    gd_ref[0] = jnp.sum(d_in, axis=0, keepdims=True)
    ga_ref[0] = jnp.sum(d_rate * dt, axis=0, keepdims=True) * neg


def bc_back_kernel(keep_ref, dbc_ref, bcin_ref, taps_ref, bias_ref, out_ref, gt_ref, gb_ref, ext, pad):
    keep = keep_ref[pl.program_id(0)]
    width = bcin_ref.shape[1]
    pad[0:HALO, :] = jnp.zeros((HALO, width), F32)
    pad[HALO + BLOCK :, :] = jnp.zeros((HALO, width), F32)
    ext[...] = bcin_ref[...].astype(F32)
    d_in, g_taps, g_bias = conv_back(
        ext, pad, dbc_ref[...].astype(F32), taps_ref[...], bias_ref[...], keep
    )
    out_ref[...] = d_in.astype(BF16)
    for tap_at in range(4):
        gt_ref[0, tap_at : tap_at + 1, :] = g_taps[tap_at]
    gb_ref[0] = g_bias


def run_kernel(body, name, grid, scalars, operands, in_specs, out_specs, out_shape, scratch=()):
    return pl.pallas_call(
        body,
        grid_spec=pltpu.PrefetchScalarGridSpec(
            num_scalar_prefetch=len(scalars),
            grid=grid,
            in_specs=in_specs,
            out_specs=out_specs,
            scratch_shapes=list(scratch),
        ),
        out_shape=out_shape,
        name=name,
    )(*scalars, *operands)


def pad_lanes(value, width):
    extra = width - value.shape[-1]
    if extra == 0:
        return value
    return jnp.pad(value, [(0, 0)] * (value.ndim - 1) + [(0, extra)])


def per_device(
    hidden,
    cotangent,
    z_proj,
    x_proj,
    bc_proj,
    dt_proj,
    out_proj,
    conv_x,
    conv_x_bias,
    conv_bc,
    conv_bc_bias,
    dt_bias,
    a_log,
    d_skip,
    norm_gain,
    gate_gain,
    lengths,
    dealing,
):
    n = lax.axis_size("seq")
    n_head = lax.axis_size("head")
    seq_at = lax.axis_index("seq")
    head_at = lax.axis_index("head")
    micro = lengths.shape[0]
    width = z_proj.shape[1]
    bc_loc = bc_proj.shape[1]
    heads = dt_proj.shape[1]
    portion = MODEL_WIDTH // n_head
    own = MODEL_WIDTH // n
    planes = n // 4
    nb = STATE // n
    rows = micro * BLOCK
    span = BLOCK + HALO
    rows_ext = micro * span
    bc_pad = -(-bc_loc // LANES) * LANES
    in_width = width + bc_pad + LANES

    def swap(value, bit):
        return lax.ppermute(value, "seq", [(i, i ^ bit) for i in range(n)])

    def plane_shift(value, k):
        return lax.ppermute(value, "seq", [(i, (i + 4 * k) % n) for i in range(n)])

    def all_to_all(value):
        return lax.all_to_all(value, "seq", 0, 0, tiled=False)

    order = jnp.arange(n, dtype=jnp.int32)
    run_ends = jnp.cumsum(lengths, axis=1)
    first = jnp.any((run_ends - lengths)[:, :, None] == order[None, None, :], axis=1)
    pos = jnp.sum(jnp.where(dealing == seq_at, order[None], 0), axis=1)
    at_pos = order[None] == pos[:, None]
    keep = 1.0 - jnp.sum(jnp.where(at_pos, first, False).astype(F32), axis=1)
    pred_dev = jnp.sum(jnp.where(order[None] == jnp.maximum(pos - 1, 0)[:, None], dealing, 0), axis=1)
    succ_dev = jnp.sum(jnp.where(order[None] == jnp.minimum(pos + 1, n - 1)[:, None], dealing, 0), axis=1)
    has_next = (pos + 1 < n).astype(F32)
    first_flat = first.astype(jnp.int32).reshape(-1)
    deal_flat = dealing.reshape(-1)
    z_at, near_at = seq_at // 4, seq_at % 4
    from_places = jnp.stack(
        [((z_at - k) % planes) * 4 + (near_at ^ near) for k in range(planes) for near in range(4)]
    ).astype(jnp.int32)
    to_places = jnp.stack(
        [((z_at + k) % planes) * 4 + (near_at ^ near) for k in range(planes) for near in range(4)]
    ).astype(jnp.int32)

    def gather_rows(block):
        layers = [block] + [plane_shift(block, k) for k in range(1, planes)]
        blocks = []
        for k, layer in enumerate(layers):
            by_x, by_y = swap(layer, 1), swap(layer, 2)
            far = swap(by_y, 1) if k % 2 == 0 else swap(by_x, 2)
            blocks += [layer, by_x, by_y, far]
        return assemble(blocks, from_places)

    def scatter_rows(grad):
        x_send, x_keep0, x_keep1, y_send, y_keep0, y_keep1 = take_apart(grad, to_places, n)
        x_got, y_got = swap(x_send, 1), swap(y_send, 2)
        y_next = (x_keep1.astype(F32) + x_got[:, 1].astype(F32)).astype(BF16)
        x_next = (y_keep1.astype(F32) + y_got[:, 1].astype(F32)).astype(BF16)
        y_last, x_last = swap(y_next, 2), swap(x_next, 1)
        even = x_keep0.astype(F32) + x_got[:, 0].astype(F32) + y_last.astype(F32)
        odd = y_keep0.astype(F32) + y_got[:, 0].astype(F32) + x_last.astype(F32)
        total = even[0]
        for k in range(1, planes):
            part = (odd if k % 2 else even)[k // 2]
            total = total + plane_shift(part.astype(BF16), k).astype(F32)
        return total

    group = jnp.concatenate([x_proj, pad_lanes(bc_proj, bc_pad), pad_lanes(dt_proj, LANES)], axis=1)
    w_in = gather_rows(group)
    w_z = gather_rows(z_proj)
    w_out = lax.all_gather(out_proj, "seq", axis=0, tiled=True)
    hidden3 = hidden.reshape(micro, BLOCK, MODEL_WIDTH)
    tails = hidden3[:, BLOCK - 3 :].reshape(micro * 3, MODEL_WIDTH)
    tails_all = all_to_all(jnp.broadcast_to(tails[None], (n, micro * 3, MODEL_WIDTH)))
    halo = jnp.stack(
        [
            lax.dynamic_slice(tails_all, (pred_dev[m], 3 * m, 0), (1, 3, MODEL_WIDTH))[0]
            for m in range(micro)
        ]
    )

    def normalize(value):
        value = value.astype(F32)
        root = lax.rsqrt(jnp.mean(value * value, axis=-1, keepdims=True) + EPSILON)
        return value * root, root

    x_hat, inv_rms = normalize(hidden)
    normed = (x_hat * norm_gain).astype(BF16)
    normed_halo = (normalize(halo)[0] * norm_gain).astype(BF16)
    normed_ext = jnp.concatenate(
        [
            jnp.zeros((micro, HALO - 3, MODEL_WIDTH), BF16),
            normed_halo,
            normed.reshape(micro, BLOCK, MODEL_WIDTH),
        ],
        axis=1,
    ).reshape(rows_ext, MODEL_WIDTH)

    neg_rate = pad_lanes(-jnp.exp(a_log)[None], LANES)
    dtb = pad_lanes(dt_bias[None], LANES)
    skip = jnp.repeat(d_skip, HDIM)[None]
    taps_bc, bias_bc = pad_lanes(conv_bc, bc_pad), pad_lanes(conv_bc_bias[None], bc_pad)
    bc_raw = dot_nn(normed_ext, w_in[:, width : width + bc_pad])
    dt_raw = dot_nn(normed_ext, w_in[:, width + bc_pad :])
    bc_in, bc_act, dt, cs, sig, cs_t = run_kernel(
        prep_kernel, "prep", (micro,), (keep,),
        (bc_raw, dt_raw, taps_bc, bias_bc, dtb, neg_rate),
        [row_block(span, bc_pad), row_block(span, LANES), whole_block(4, bc_pad), whole_block(1, bc_pad),
         whole_block(1, LANES), whole_block(1, LANES)],
        [row_block(span, bc_pad), row_block(BLOCK, bc_pad)] + [row_block(BLOCK, LANES)] * 3
        + [lead_block(LANES, BLOCK)],
        [shape_of((rows_ext, bc_pad), BF16), shape_of((rows, bc_pad), BF16)]
        + [shape_of((rows, LANES), F32)] * 3 + [shape_of((micro, LANES, BLOCK), F32)],
        [pltpu.VMEM((span, bc_pad), F32)],
    )
    bc_all = lax.all_gather(bc_act[:, :bc_loc], "head", axis=1, tiled=True)
    b_mat, c_mat = bc_all[:, :STATE], bc_all[:, STATE:]
    lam = cs.reshape(micro, BLOCK, LANES)[:, BLOCK - 1]
    lam_all = all_to_all(jnp.broadcast_to(lam[None], (n, micro, LANES))).transpose(1, 0, 2)
    tile = lane_tile(width)
    x_in, x_mix = run_kernel(
        project_kernel, "project", (width // tile,), (keep,),
        (normed_ext, w_in, conv_x, conv_x_bias[None]),
        [pl.BlockSpec((rows_ext, MODEL_WIDTH), lambda c, *_: (0, 0)),
         pl.BlockSpec((MODEL_WIDTH, tile), lambda c, *_: (0, c)),
         pl.BlockSpec((4, tile), lambda c, *_: (0, c)),
         pl.BlockSpec((1, tile), lambda c, *_: (0, c))],
        [pl.BlockSpec((rows_ext, tile), lambda c, *_: (0, c)),
         pl.BlockSpec((rows, tile), lambda c, *_: (0, c))],
        [shape_of((rows_ext, width), BF16), shape_of((rows, width), BF16)],
        [pltpu.VMEM((rows_ext, tile), F32)],
    )

    x_block = row_block(BLOCK, width)
    head_block = row_block(BLOCK, LANES)
    states_block = state_block(n, nb, width)
    states_shape = shape_of((n, micro, nb, width), BF16)

    def exchange(payload, reverse):
        got = all_to_all(payload)
        scanned = pl.pallas_call(
            lambda *refs: scan_kernel(reverse, *refs),
            grid_spec=pltpu.PrefetchScalarGridSpec(
                num_scalar_prefetch=2,
                grid=(1,),
                in_specs=[pl.BlockSpec((n, micro, nb, width), lambda m, *_: (0, 0, 0, 0)),
                          pl.BlockSpec((micro, n, LANES), lambda m, *_: (0, 0, 0))],
                out_specs=pl.BlockSpec((n, micro, nb, width), lambda m, *_: (0, 0, 0, 0)),
                scratch_shapes=[pltpu.VMEM((micro * n, width), F32)],
            ),
            out_shape=states_shape,
            name="scan_back" if reverse else "scan",
        )(deal_flat, first_flat, got, lam_all)
        return all_to_all(scanned)

    end_states = run_kernel(
        end_state_kernel, "end_state", (micro,), (),
        (x_mix, b_mat, dt, cs),
        [x_block, head_block, head_block, head_block],
        states_block, states_shape,
    )
    s_in = exchange(end_states, False)
    y_intra = run_kernel(
        intra_kernel, "intra", (micro,), (),
        (x_mix, b_mat, c_mat, dt, cs, cs_t),
        [x_block, head_block, head_block, head_block, head_block, lead_block(LANES, BLOCK)],
        x_block, shape_of((rows, width), F32),
        [pltpu.VMEM((BLOCK, BLOCK), F32)],
    )
    gate = dot_nn(normed, w_z).astype(BF16)
    d_branch = dot_nn(cotangent, w_out)
    gain = gate_gain[None]
    gain_block = whole_block(1, width)
    y, stats = run_kernel(
        stats_kernel, "stats", (micro,), (),
        (y_intra, x_mix, c_mat, cs, s_in, gate, d_branch, gain, skip),
        [x_block, x_block, head_block, head_block, states_block, x_block, x_block, gain_block, gain_block],
        [x_block, row_block(BLOCK, 2)],
        [shape_of((rows, width), F32), shape_of((rows, 2), F32)],
        [pltpu.VMEM((STATE, width), F32)],
    )
    totals = jnp.sum(lax.all_gather(stats, "head", axis=0), axis=0)
    branch, d_y, d_gate, g_gate, d_entry = run_kernel(
        gate_kernel, "gate", (micro,), (),
        (y, c_mat, cs, gate, d_branch, gain, totals),
        [x_block, head_block, head_block, x_block, x_block, gain_block, row_block(BLOCK, 2)],
        [x_block, x_block, x_block, lead_block(1, width), states_block],
        [shape_of((rows, width), BF16)] * 3 + [shape_of((micro, 1, width), F32), states_shape],
    )
    d_state = exchange(d_entry, True)

    partial_out = dot_nt(branch, w_out)
    out_piece = lax.psum_scatter(
        partial_out.astype(BF16), "head", scatter_dimension=1, tiled=True
    ).astype(F32)
    hidden_share = lax.dynamic_slice_in_dim(hidden, head_at * portion, portion, 1).astype(F32)
    block_out = (hidden_share + out_piece).astype(BF16)
    grad_out = scatter_rows(dot_tn(cotangent, branch).astype(BF16))
    grad_z = scatter_rows(dot_tn(normed, d_gate).astype(BF16))

    dx_part, db_part, dc_part, dcs_part, ddt_part, g_skip = run_kernel(
        intra_back_kernel, "intra_back", (micro,), (),
        (x_mix, d_y, b_mat, c_mat, dt, cs, cs_t, y, s_in, skip),
        [x_block, x_block, head_block, head_block, head_block, head_block, lead_block(LANES, BLOCK),
         x_block, states_block, gain_block],
        [x_block, head_block, head_block, head_block, head_block, lead_block(1, width)],
        [shape_of((rows, width), F32)] + [shape_of((rows, LANES), F32)] * 4
        + [shape_of((micro, 1, width), F32)],
        [pltpu.VMEM((BLOCK, BLOCK), F32), pltpu.VMEM((BLOCK, BLOCK), F32), pltpu.VMEM((STATE, width), F32)],
    )
    d_x, d_bc, d_dt, g_taps, g_bias, g_alog, g_dtb = run_kernel(
        state_back_kernel, "state_back", (micro,), (keep,),
        (x_mix, b_mat, dt, cs, sig, neg_rate, s_in, d_state, dx_part, db_part, dc_part, dcs_part, ddt_part,
         x_in, conv_x, conv_x_bias[None]),
        [x_block, head_block, head_block, head_block, head_block, whole_block(1, LANES), states_block,
         states_block, x_block, head_block, head_block, head_block, head_block, row_block(span, width),
         whole_block(4, width), whole_block(1, width)],
        [row_block(span, width), row_block(BLOCK, 2 * STATE), row_block(span, LANES), lead_block(4, width),
         lead_block(1, width), lead_block(1, LANES), lead_block(1, LANES)],
        [shape_of((rows_ext, width), BF16), shape_of((rows, 2 * STATE), BF16), shape_of((rows_ext, LANES), BF16),
         shape_of((micro, 4, width), F32), shape_of((micro, 1, width), F32), shape_of((micro, 1, LANES), F32),
         shape_of((micro, 1, LANES), F32)],
        [pltpu.VMEM((STATE, width), F32), pltpu.VMEM((STATE, width), F32), pltpu.VMEM((span, tile), F32),
         pltpu.VMEM((span + HALO, tile), F32)],
    )
    d_bc_own = lax.psum_scatter(d_bc, "head", scatter_dimension=1, tiled=True)
    d_bc_ext, g_taps_bc, g_bias_bc = run_kernel(
        bc_back_kernel, "bc_back", (micro,), (keep,),
        (pad_lanes(d_bc_own, bc_pad), bc_in, taps_bc, bias_bc),
        [row_block(BLOCK, bc_pad), row_block(span, bc_pad), whole_block(4, bc_pad), whole_block(1, bc_pad)],
        [row_block(span, bc_pad), lead_block(4, bc_pad), lead_block(1, bc_pad)],
        [shape_of((rows_ext, bc_pad), BF16), shape_of((micro, 4, bc_pad), F32), shape_of((micro, 1, bc_pad), F32)],
        [pltpu.VMEM((span, bc_pad), F32), pltpu.VMEM((span + HALO, bc_pad), F32)],
    )
    d_group = jnp.concatenate([d_x, d_bc_ext, d_dt], axis=1)
    grad_in = scatter_rows(dot_tn(normed_ext, d_group).astype(BF16))

    d_normed_ext = dot_nt(d_group, w_in).reshape(micro, span, MODEL_WIDTH)
    edges = d_normed_ext[:, HALO - 3 : HALO].reshape(micro * 3, MODEL_WIDTH).astype(BF16)
    edges_all = all_to_all(jnp.broadcast_to(edges[None], (n, micro * 3, MODEL_WIDTH)))
    incoming = jnp.stack(
        [
            lax.dynamic_slice(edges_all, (succ_dev[m], 3 * m, 0), (1, 3, MODEL_WIDTH))[0].astype(F32)
            * has_next[m]
            for m in range(micro)
        ]
    )
    d_normed = dot_nt(d_gate, w_z) + (
        d_normed_ext[:, HALO:] + jnp.pad(incoming, ((0, 0), (BLOCK - 3, 0), (0, 0)))
    ).reshape(rows, MODEL_WIDTH)
    piece = lax.psum_scatter(
        d_normed.astype(BF16), "head", scatter_dimension=1, tiled=True
    ).astype(F32)
    x_hat_share = hidden_share * inv_rms
    gain_share = lax.dynamic_slice_in_dim(norm_gain, head_at * portion, portion, 0)
    d_hat = piece * gain_share
    g_norm = jnp.sum(piece * x_hat_share, axis=0)
    row_stat = jnp.sum(
        lax.all_gather(jnp.sum(d_hat * x_hat_share, axis=1), "head", axis=0), axis=0
    )
    cot_share = lax.dynamic_slice_in_dim(cotangent, head_at * portion, portion, 1).astype(F32)
    grad_hidden = inv_rms * (d_hat - x_hat_share * (row_stat / MODEL_WIDTH)[:, None]) + cot_share

    small = [
        jnp.sum(g_taps, axis=0),
        jnp.sum(g_bias, axis=0),
        jnp.sum(g_taps_bc, axis=0)[:, :bc_loc],
        jnp.sum(g_bias_bc, axis=0)[:, :bc_loc],
        jnp.sum(g_dtb, axis=0)[:, :heads],
        jnp.sum(g_alog, axis=0)[:, :heads],
        jnp.sum(jnp.sum(g_skip, axis=0).reshape(heads, HDIM), axis=1),
        g_norm,
        jnp.sum(g_gate, axis=0),
    ]
    flat = jnp.concatenate([item.reshape(-1) for item in small])
    length = flat.shape[0]
    flat = jnp.pad(flat, (0, -length % 1024)).reshape(-1, LANES)
    bit = 1
    while bit < n:
        flat = flat + swap(flat, bit)
        bit *= 2
    flat = flat.reshape(-1)
    sums, at = [], 0
    for item in small:
        sums.append(flat[at : at + item.size].reshape(item.shape))
        at += item.size
    return (
        block_out,
        grad_hidden,
        grad_z,
        grad_in[:, :width],
        grad_in[:, width : width + bc_loc],
        grad_in[:, width + bc_pad : width + bc_pad + heads],
        grad_out,
        sums[0],
        sums[1].reshape(-1),
        sums[2],
        sums[3].reshape(-1),
        sums[4].reshape(-1),
        sums[5].reshape(-1),
        sums[6],
        sums[7],
        sums[8].reshape(-1),
    )


def solution(mesh):
    return jax.shard_map(
        per_device,
        mesh=mesh,
        in_specs=(
            P("seq", None),
            P("seq", None),
            P("seq", "head"),
            P("seq", "head"),
            P("seq", "head"),
            P("seq", "head"),
            P("seq", "head"),
            P(None, "head"),
            P("head"),
            P(None, "head"),
            P("head"),
            P("head"),
            P("head"),
            P("head"),
            P(),
            P("head"),
            P(),
            P(),
        ),
        out_specs=(
            P("seq", "head"),
            P("seq", "head"),
            P("seq", "head"),
            P("seq", "head"),
            P("seq", "head"),
            P("seq", "head"),
            P("seq", "head"),
            P(None, "head"),
            P("head"),
            P(None, "head"),
            P("head"),
            P("head"),
            P("head"),
            P("head"),
            P("head"),
            P("head"),
        ),
        check_vma=False,
    )
```
